256 devices in a mesh: dp: 32 (over z, x), tensor: 8 (over y, core).
Axes of the slice: x: 4, y: 4, z: 8, core: 2. Of those that a mesh axis runs over, the one named last changes fastest.
Arguments:
- tokens: bfloat16 [32768, 8192], P('dp', 'tensor'), may hold values from -6 to 6
- key_value_weight: bfloat16 [8192, 8, 256], P('tensor'), may hold values from -0.09375 to 0.09375
- key_value_bias: bfloat16 [8, 256], P('tensor'), may hold values from -3 to 3
- adapter_down_weight: bfloat16 [64, 8192, 128], P('dp', 'tensor'), may hold values from -0.0625 to 0.0625
- adapter_up_weight: bfloat16 [64, 8, 2, 64, 128], P('dp', 'tensor'), may hold values from -0.75 to 0.75
- conversation_adapter: int32 [512], replicated, may hold values from 0 to 63, as said below
- adapter_slot_table: int32 [64], replicated, may hold values from 0 to 63, as said below
- span_length: int32 [512], P('dp'), may hold values from 40 to 64, as said below
- context_length: int32 [512], P('dp'), may hold values from 0 to 4096
Outputs:
- new_kv: bfloat16 [8, 32768, 256], P('tensor', 'dp')
The draws below stay inside these ranges and needn't reach their ends.
Inputs may be any that keep to these rules, and one draw needn't show every extreme that they name: `conversation_adapter`: the 16 conversations of each index of dp use adapters whose slots lie on 16 different owners (owner of slot p: p // 2), so an owner serves at most one conversation of each index of dp, and some owner serves one of every index. `adapter_slot_table`: A permutation: every storage slot holds exactly one adapter. `span_length`: every index of dp has a conversation whose span fills all 64 slots.
All inputs are finite; a program needn't handle non-finite values.
Results may differ from the reference program's by a relative error of at most 0.019.
Values may be sent and summed in bfloat16 or wider, within the bound.
No kernel may reach another device: no remote copies, remote signals or barrier semaphores. Data moves between devices by JAX's collectives and lax.ppermute only.
A program may use at most 128 MiB of HBM per device.

```python
import math
import jax
import jax.numpy as jnp
from jax import lax

MODEL_WIDTH = 8192
KEY_VALUE_HEADS = 8
HEAD_SIZE = 128
ADAPTER_RANK = 64
ADP_DEV = 2
SPAN = 64
CTX = 4096
CONV_DP = 16
CONVS = 512
TOKENS = 32768
ADAPTER_COUNT = 64
N_DP = 32
N_TENSOR = 8


def routing_draw(key):
    key = jax.random.fold_in(key, 4242)
    key_perm, key_hot, key_pick, key_local = jax.random.split(key, 4)
    slot_of = jax.random.permutation(key_perm, ADP_DEV * N_DP).astype(jnp.int32)
    adapter_at = jnp.argsort(slot_of).astype(jnp.int32)
    hot_owner = jax.random.randint(key_hot, (), 0, N_DP).astype(jnp.int32)
    group_keys = jax.random.split(key_pick, N_DP)

    def one_group(group_key):
        key_order, key_roll = jax.random.split(group_key)
        others = jax.random.permutation(key_order, N_DP - 1).astype(jnp.int32)[:CONV_DP - 1]
        owners = jnp.concatenate([hot_owner[None], (hot_owner + 1 + others) % N_DP])
        roll_by = jax.random.randint(key_roll, (), 0, CONV_DP)
        return jnp.roll(owners, roll_by)
    owners = jax.vmap(one_group)(group_keys)
    local_pick = jax.random.randint(key_local, (N_DP, CONV_DP), 0, ADP_DEV).astype(jnp.int32)
    adapters = adapter_at[owners * ADP_DEV + local_pick]
    return (slot_of, adapters.reshape(-1).astype(jnp.int32), (owners == hot_owner).reshape(-1))


def draw_conversation_adapter(key, part):
    return routing_draw(key)[1]


def draw_adapter_slot_table(key, part):
    return routing_draw(key)[0]


def draw_span_length(key, part):
    hot_rows = routing_draw(key)[2]
    drawn = jax.random.randint(jax.random.fold_in(key, 77), (CONV_DP * N_DP,), SPAN * 5 // 8, SPAN + 1).astype(jnp.int32)
    return jnp.where(hot_rows, SPAN, drawn).astype(jnp.int32)


def touch_ends(entries, rng, least, high):
    longest = entries.shape.index(max(entries.shape))
    spots = []
    for shift in (0, 1):
        where = [jax.random.randint(jax.random.fold_in(rng, axis), (), 0, length) for axis, length in enumerate(entries.shape)]
        where[longest] = (where[longest] + shift) % entries.shape[longest]
        spots.append(tuple(where))
    return entries.at[spots[0]].set(least).at[spots[1]].set(high)


def with_spikes(entries, own_key, source, target, parts, factor):
    def block_of(dim):
        return (jnp.arange(entries.shape[dim]) // (entries.shape[dim] // parts)).reshape((-1,) + (1,) * (entries.ndim - 1 - dim))

    near = jax.random.permutation(own_key, parts)[block_of(target)]
    other_side = (block_of(target) + parts // 2) % parts
    return jnp.where((block_of(source) == near) | (block_of(source) == other_side), factor * entries, entries)


def shard_levels(own_key, extent, cuts, least, largest):
    def one(axis_at, shards_of):
        heights = jax.random.uniform(jax.random.fold_in(jax.random.fold_in(own_key, 6), axis_at), (shards_of,), jnp.float32, least / len(cuts), largest / len(cuts))
        return jnp.repeat(jnp.exp(heights), extent[axis_at] // shards_of).reshape((-1,) + (1,) * (len(extent) - axis_at - 1))

    level = one(*cuts[0])
    for cut in cuts[1:]:
        level = level * one(*cut)
    return level


def scatter_about(stream_key, dims, spread, most, cuts=(), held_as=jnp.bfloat16):
    array = spread * jax.random.normal(stream_key, dims, jnp.float32)
    if cuts:
        array = array * shard_levels(stream_key, dims, cuts, -0.22, 0.18)
    return jnp.clip(array, -most, most).astype(held_as)


def noise_with(rng, dims, deviation, limit, shards, heavy, kind=jnp.bfloat16):
    values = deviation * jax.random.normal(rng, dims, jnp.float32)
    if shards:
        values = values * shard_levels(rng, dims, shards, -0.22, 0.18)
    return jnp.clip(with_spikes(values, jax.random.fold_in(rng, 3), *heavy), -limit, limit).astype(kind)


def setup_inputs(seed: int = 0) -> dict:
    arg_keys = jax.random.split(jax.random.key(seed), 10)
    return {
        "tokens": scatter_about(arg_keys[0], (TOKENS, MODEL_WIDTH), 1.0, 6.0, ((0, 32), (1, 8))),
        "key_value_weight": noise_with(arg_keys[1], (MODEL_WIDTH, KEY_VALUE_HEADS, 2 * HEAD_SIZE), MODEL_WIDTH ** -0.5, 0.09375, ((0, 8),), (0, 1, 8, 2.0)),
        "key_value_bias": scatter_about(arg_keys[2], (KEY_VALUE_HEADS, 2 * HEAD_SIZE), 0.5, 3.0, ((0, 8),)),
        "adapter_down_weight": scatter_about(arg_keys[3], (ADAPTER_COUNT, MODEL_WIDTH, 2 * ADAPTER_RANK), MODEL_WIDTH ** -0.5, 0.0625, ((0, 32), (1, 8))),
        "adapter_up_weight": scatter_about(arg_keys[4], (ADAPTER_COUNT, KEY_VALUE_HEADS, 2, ADAPTER_RANK, HEAD_SIZE), ADAPTER_RANK ** -0.5, 0.75, ((0, 32), (1, 8))),
        "conversation_adapter": draw_conversation_adapter(jax.random.fold_in(arg_keys[9], 71), 0),
        "adapter_slot_table": draw_adapter_slot_table(jax.random.fold_in(arg_keys[9], 71), 0),
        "span_length": draw_span_length(jax.random.fold_in(arg_keys[9], 71), 0),
        "context_length": touch_ends(jax.random.randint(arg_keys[8], (CONVS,), 0, CTX + 1), jax.random.fold_in(arg_keys[8], 1), 0, CTX).astype(jnp.int32),
    }


rope_base = 1000000.0


def rotary(key_part, positions):
    half_dim = key_part.shape[-1] // 2
    inverse_freq = jnp.exp(jnp.arange(half_dim, dtype=jnp.float32) * (-2.0 * math.log(rope_base) / key_part.shape[-1]))
    angles = positions[:, None] * inverse_freq[None, :]
    angles = jnp.concatenate([angles, angles], axis=-1)
    turned = jnp.concatenate([-key_part[..., half_dim:], key_part[..., :half_dim]], axis=-1)
    return key_part * jnp.cos(angles) + turned * jnp.sin(angles)


def reference(tokens, key_value_weight, key_value_bias, adapter_down_weight, adapter_up_weight, conversation_adapter, adapter_slot_table, span_length, context_length):
    slice_width = MODEL_WIDTH // N_TENSOR
    flat_weight = key_value_weight.reshape(MODEL_WIDTH, KEY_VALUE_HEADS * 2 * HEAD_SIZE)
    base_sum = jnp.zeros((TOKENS, KEY_VALUE_HEADS * 2 * HEAD_SIZE), jnp.float32)
    for stripe in range(N_TENSOR):
        partial_sum = jnp.dot(tokens[:, stripe * slice_width:(stripe + 1) * slice_width],
                              flat_weight[stripe * slice_width:(stripe + 1) * slice_width],
                              preferred_element_type=jnp.float32)
        rounded = lax.optimization_barrier(partial_sum.astype(jnp.bfloat16))
        base_sum = base_sum + rounded.astype(jnp.float32)
    storage = adapter_slot_table[conversation_adapter].astype(jnp.int32)

    def adapt_one(item):
        conversation_rows, storage_slot_index = item
        rank_activation = jnp.dot(conversation_rows, adapter_down_weight[storage_slot_index], preferred_element_type=jnp.float32).astype(jnp.bfloat16)
        up_weight_block = adapter_up_weight[storage_slot_index].astype(jnp.float32)
        rank_halves = rank_activation.astype(jnp.float32).reshape(SPAN, 2, ADAPTER_RANK)
        adapter_delta = jnp.einsum("oiu,kiuq->okiq", rank_halves, up_weight_block)
        return adapter_delta.astype(jnp.bfloat16)

    deltas = lax.map(adapt_one, (tokens.reshape(CONVS, SPAN, MODEL_WIDTH), storage))
    projected = base_sum.reshape(TOKENS, KEY_VALUE_HEADS, 2 * HEAD_SIZE) + key_value_bias.astype(jnp.float32)[None, :, :]
    projected = projected + deltas.reshape(TOKENS, KEY_VALUE_HEADS, 2 * HEAD_SIZE).astype(jnp.float32)
    projected = jnp.transpose(projected, (1, 0, 2))
    positions = (context_length[:, None] + jnp.arange(SPAN, dtype=jnp.int32)[None, :]).reshape(TOKENS).astype(jnp.float32)
    rotated = rotary(projected[..., :HEAD_SIZE], positions)
    live_mask = (jnp.arange(SPAN, dtype=jnp.int32)[None, :] < span_length[:, None]).reshape(TOKENS)
    joined = jnp.concatenate([rotated, projected[..., HEAD_SIZE:]], axis=-1)
    return jnp.where(live_mask[None, :, None], joined, 0.0).astype(jnp.bfloat16)
```

```python
import functools
import math

import jax
import jax.numpy as jnp
from jax import lax
from jax.experimental import pallas as pl
from jax.experimental.pallas import tpu as pltpu
from jax.sharding import PartitionSpec as P

rope_base = 1000000.0
NZ, NX, NY, NC = 8, 4, 4, 2
BF = jnp.bfloat16
F32 = jnp.float32


def shift_x(v, s):
    pairs = [(z * NX + x, z * NX + (x + s) % NX) for z in range(NZ) for x in range(NX)]
    return lax.ppermute(v, "dp", pairs)


def shift_z(v, s):
    pairs = [(z * NX + x, ((z + s) % NZ) * NX + x) for z in range(NZ) for x in range(NX)]
    return lax.ppermute(v, "dp", pairs)


def shift_y(v, s):
    pairs = [(y * NC + c, ((y + s) % NY) * NC + c) for y in range(NY) for c in range(NC)]
    return lax.ppermute(v, "tensor", pairs)


def swap_core(v):
    return lax.ppermute(v, "tensor", [(t, t ^ 1) for t in range(NY * NC)])


def slot_of(ca_ref, table_ref, index, z, x):
    storage = table_ref[ca_ref[index]]
    owner = storage >> 1
    across = ((owner & (NX - 1)) - x) & (NX - 1)
    along = ((owner >> 2) - z) & (NZ - 1)
    return across, along, storage & 1


def pack_kernel(ca_ref, table_ref, tok_ref, o0, o1, o2, o3, sem):
    d = lax.axis_index("dp")
    z, x = d >> 2, d & (NX - 1)
    convs = tok_ref.shape[0]

    def step(i, carry):
        across, along, _ = slot_of(ca_ref, table_ref, d * convs + i, z, x)
        for r, out in enumerate((o0, o1, o2, o3)):

            @pl.when(across == r)
            def _():
                pltpu.make_async_copy(tok_ref.at[i], out.at[along], sem).start()

        return carry

    lax.fori_loop(0, convs, step, 0)
    pltpu.make_async_copy(tok_ref, tok_ref, sem).wait()


def plan_kernel(ca_ref, table_ref, choice_ref, place_ref):
    d = lax.axis_index("dp")
    z, x = d >> 2, d & (NX - 1)
    convs = place_ref.shape[0]

    def clear(i, carry):
        choice_ref[i] = 0
        return carry

    lax.fori_loop(0, NX * NZ, clear, 0)

    def step(i, carry):
        across, along, _ = slot_of(ca_ref, table_ref, d * convs + i, z, x)
        place_ref[i] = across * NZ + along
        for r in range(NX):
            xs = (x - r) & (NX - 1)
            across_r, along_r, which = slot_of(ca_ref, table_ref, (z * NX + xs) * convs + i, z, xs)

            @pl.when(across_r == r)
            def _():
                choice_ref[r * NZ + along_r] = which

        return carry

    lax.fori_loop(0, convs, step, 0)


def rank_kernel(choice_ref, *refs):
    toks = refs[0:4]
    stacks = refs[4:13]
    ranks = refs[13:17]
    ups = refs[17:21]
    depth = toks[0].shape[2]
    width = stacks[0].shape[2]
    rows = toks[0].shape[1]
    for k in range(NZ):
        tok = jnp.concatenate([t[k] for t in toks], axis=0)
        if k == NZ // 2:
            first, second = stacks[k], stacks[NZ]
            w = jnp.concatenate([first[:depth], second[:depth]], axis=1)
        else:
            w = jnp.concatenate([stacks[k][0, :depth], stacks[k][1, :depth]], axis=1)
        res = jnp.dot(tok, w, preferred_element_type=F32)
        for r in range(NX):
            which = choice_ref[r * NZ + k]
            part = res[r * rows : (r + 1) * rows]
            ranks[r][k] = jnp.where(which == 1, part[:, width:], part[:, :width]).astype(BF)
            if k == NZ // 2:
                ups[r][k] = jnp.where(which == 1, second[depth:], first[depth:])
            else:
                ups[r][k] = stacks[k][which, depth:]


def pick(sources, place, count):
    across, along = place >> 3, place & (NZ - 1)
    value = sources[0][along]
    for r in range(1, count):
        value = jnp.where(across == r, sources[r][along], value)
    return value


def unslot_kernel(place_ref, g0, g1, g2, g3, keep, send):
    c = lax.axis_index("tensor") & 1
    half = keep.shape[0]
    for j in range(half):
        keep[j] = pick((g0, g1, g2, g3), place_ref[c * half + j], NX)
        send[j] = pick((g0, g1, g2, g3), place_ref[(1 - c) * half + j], NX)


def final_kernel(
    place_ref, span_ref, mine, other, u0, u1, u2, u3, b0, b1, b2, b3, bias, cosine, sine, out
):
    c = lax.axis_index("tensor") & 1
    step = pl.program_id(0)
    half, rows, _ = mine.shape
    rank = mine.shape[2] // 2
    per = out.shape[1] // rows
    head = out.shape[2] // 2
    for j in range(per):
        conv = step * per + j
        here = conv & (half - 1)
        act = jnp.where((conv >> 3) == c, mine[here], other[here])
        up = pick((u0, u1, u2, u3), place_ref[conv], NX)
        key_delta = jnp.dot(act[:, :rank], up[:rank], preferred_element_type=F32).astype(BF)
        value_delta = jnp.dot(act[:, rank:], up[rank:], preferred_element_type=F32).astype(BF)
        spot = pl.ds(j * rows, rows)
        base = b0[spot].astype(F32) + b1[spot].astype(F32)
        base = base + b2[spot].astype(F32) + b3[spot].astype(F32)
        base = base + bias[0:1].astype(F32)
        key = base[:, :head] + key_delta.astype(F32)
        value = base[:, head:] + value_delta.astype(F32)
        key = key * cosine[spot] + pltpu.roll(key, head // 2, 1) * sine[spot]
        live = lax.broadcasted_iota(jnp.int32, (rows, head), 0) < span_ref[conv]
        out[0, spot, :head] = jnp.where(live, key, 0.0).astype(BF)
        out[0, spot, head:] = jnp.where(live, value, 0.0).astype(BF)


VMEM_SPEC = pl.BlockSpec(memory_space=pltpu.VMEM)
ANY_SPEC = pl.BlockSpec(memory_space=pl.ANY)
SMEM_SPEC = pl.BlockSpec(memory_space=pltpu.SMEM)


def body(
    tokens,
    key_value_weight,
    key_value_bias,
    adapter_down_weight,
    adapter_up_weight,
    conversation_adapter,
    adapter_slot_table,
    span_length,
    context_length,
):
    convs = span_length.shape[0]
    total, depth = tokens.shape
    rows = total // convs
    heads, width = key_value_weight.shape[1:]
    head = width // 2
    double_rank = adapter_down_weight.shape[2]
    t = lax.axis_index("tensor")
    y, c = t // NC, t % NC
    half = convs // 2

    slots = jax.ShapeDtypeStruct((NZ, rows, depth), BF)
    packed = pl.pallas_call(
        pack_kernel,
        out_shape=[slots] * NX,
        in_specs=[SMEM_SPEC, SMEM_SPEC, ANY_SPEC],
        out_specs=[ANY_SPEC] * NX,
        scratch_shapes=[pltpu.SemaphoreType.DMA],
        name="pack",
    )(conversation_adapter, adapter_slot_table, tokens.reshape(convs, rows, depth))
    got = [packed[0]] + [shift_x(packed[r], r) for r in range(1, NX)]

    stack = jnp.concatenate(
        [
            adapter_down_weight,
            adapter_up_weight.reshape(adapter_up_weight.shape[0], double_rank, head),
        ],
        axis=1,
    )
    f1, b1 = shift_z(stack, 1), shift_z(stack, -1)
    f2, b2 = shift_z(f1, 1), shift_z(b1, -1)
    f3, b3 = shift_z(f2, 1), shift_z(b2, -1)
    f4, b4 = shift_z(f3[0], 1), shift_z(b3[1], -1)
    stacks = [stack, b1, b2, b3, f4, f3, f2, f1, b4]

    choice, place = pl.pallas_call(
        plan_kernel,
        out_shape=[
            jax.ShapeDtypeStruct((NX * NZ,), jnp.int32),
            jax.ShapeDtypeStruct((convs,), jnp.int32),
        ],
        in_specs=[SMEM_SPEC, SMEM_SPEC],
        out_specs=[SMEM_SPEC, SMEM_SPEC],
        name="plan",
    )(conversation_adapter, adapter_slot_table)

    part = jnp.einsum("td,dhe->hte", tokens, key_value_weight, preferred_element_type=F32)
    part = part.astype(BF).reshape(NY, NC, total, width)
    keep = lax.dynamic_index_in_dim(part, c, 1, keepdims=False)
    send = lax.dynamic_index_in_dim(part, 1 - c, 1, keepdims=False)
    pair = (keep.astype(F32) + swap_core(send).astype(F32)).astype(BF)
    bases = [lax.dynamic_index_in_dim(pair, y, 0, keepdims=False)]
    for s in range(1, NY):
        bases.append(shift_y(lax.dynamic_index_in_dim(pair, (y + s) % NY, 0, keepdims=False), s))

    positions = (
        (context_length[:, None] + jnp.arange(rows, dtype=jnp.int32)[None, :])
        .reshape(-1)
        .astype(F32)
    )
    inverse_freq = jnp.exp(
        jnp.arange(head // 2, dtype=F32) * (-2.0 * math.log(rope_base) / head)
    )
    angles = positions[:, None] * inverse_freq[None, :]
    cosine, sine = jnp.cos(angles), jnp.sin(angles)
    cosine = jnp.concatenate([cosine, cosine], axis=-1)
    sine = jnp.concatenate([-sine, sine], axis=-1)

    small = jax.ShapeDtypeStruct((NZ, rows, double_rank), BF)
    blocks = jax.ShapeDtypeStruct((NZ, double_rank, head), BF)
    results = pl.pallas_call(
        rank_kernel,
        out_shape=[small] * NX + [blocks] * NX,
        in_specs=[SMEM_SPEC] + [VMEM_SPEC] * 13,
        out_specs=[VMEM_SPEC] * 8,
        compiler_params=pltpu.CompilerParams(vmem_limit_bytes=40 * 1024 * 1024),
        name="rank",
    )(choice, *got, *stacks)
    ranks, ups = results[:NX], results[NX:]
    back = [ranks[0]] + [shift_x(ranks[r], -r) for r in range(1, NX)]

    kept = jax.ShapeDtypeStruct((half, rows, double_rank), BF)
    keep_r, send_r = pl.pallas_call(
        unslot_kernel,
        out_shape=[kept, kept],
        in_specs=[SMEM_SPEC] + [VMEM_SPEC] * 4,
        out_specs=[VMEM_SPEC] * 2,
        name="unslot",
    )(place, *back)
    mine = (keep_r.astype(F32) + swap_core(send_r).astype(F32)).astype(BF)
    others = [shift_y(mine, s) for s in range(1, NY)]
    total_rank = mine.astype(F32)
    for o in others:
        total_rank = total_rank + o.astype(F32)
    mine = total_rank.astype(BF)
    other = swap_core(mine)
    ups_late = lax.optimization_barrier((back, list(ups)))[1]
    up_back = [ups_late[0]] + [shift_x(ups_late[r], -r) for r in range(1, NX)]

    steps = 4
    base_spec = pl.BlockSpec((total // steps, width), lambda i, *_: (i, 0))
    trig_spec = pl.BlockSpec((total // steps, head), lambda i, *_: (i, 0))
    full = lambda a: pl.BlockSpec(a.shape, lambda i, *_: (0,) * a.ndim)
    return pl.pallas_call(
        final_kernel,
        out_shape=jax.ShapeDtypeStruct((1, total, width), BF),
        grid_spec=pltpu.PrefetchScalarGridSpec(
            num_scalar_prefetch=2,
            grid=(steps,),
            in_specs=[full(mine), full(other)]
            + [full(u) for u in up_back]
            + [base_spec] * 4
            + [full(key_value_bias), trig_spec, trig_spec],
            out_specs=pl.BlockSpec((1, total // steps, width), lambda i, *_: (0, i, 0)),
        ),
        name="final",
    )(place, span_length, mine, other, *up_back, *bases, key_value_bias, cosine, sine)


def solution(mesh):
    placed = (
        P("dp", "tensor"),
        P("tensor", None, None),
        P("tensor", None),
        P("dp", "tensor", None),
        P("dp", "tensor", None, None, None),
        P(),
        P(),
        P("dp"),
        P("dp"),
    )
    return jax.shard_map(
        body, mesh=mesh, in_specs=placed, out_specs=P("tensor", "dp", None), check_vma=False
    )
```

```python
import functools
import math

import jax
import jax.numpy as jnp
from jax import lax
from jax.experimental import pallas as pl
from jax.experimental.pallas import tpu as pltpu
from jax.sharding import PartitionSpec as P

rope_base = 1000000.0
NZ, NX, NY, NC = 8, 4, 4, 2
BF = jnp.bfloat16
F32 = jnp.float32


def shift_z(v, s):
    pairs = [(z * NX + x, ((z + s) % NZ) * NX + x) for z in range(NZ) for x in range(NX)]
    return lax.ppermute(v, "dp", pairs)


def shift_y(v, s):
    pairs = [(y * NC + c, ((y + s) % NY) * NC + c) for y in range(NY) for c in range(NC)]
    return lax.ppermute(v, "tensor", pairs)


def swap_core(v):
    return lax.ppermute(v, "tensor", [(t, t ^ 1) for t in range(NY * NC)])


def exchange_x(v):
    groups = [[z * NX + x for x in range(NX)] for z in range(NZ)]
    return lax.all_to_all(v, "dp", 0, 0, tiled=True, axis_index_groups=groups)


def slot_of(ca_ref, table_ref, index, z):
    storage = table_ref[ca_ref[index]]
    owner = storage >> 1
    column = owner & (NX - 1)
    along = ((owner >> 2) - z) & (NZ - 1)
    return column, column * NZ + along, storage & 1


def pack_kernel(ca_ref, table_ref, tok_ref, out_ref, sem):
    d = lax.axis_index("dp")
    convs = tok_ref.shape[0]

    def step(i, carry):
        _, slot, _ = slot_of(ca_ref, table_ref, d * convs + i, d >> 2)
        pltpu.make_async_copy(tok_ref.at[i], out_ref.at[slot], sem).start()
        return carry

    lax.fori_loop(0, convs, step, 0)
    pltpu.make_async_copy(tok_ref, tok_ref, sem).wait()


def plan_kernel(ca_ref, table_ref, choice_ref, place_ref):
    d = lax.axis_index("dp")
    z, x = d >> 2, d & (NX - 1)
    convs = place_ref.shape[0]

    def clear(i, carry):
        choice_ref[i] = 0
        return carry

    lax.fori_loop(0, NX * NZ, clear, 0)

    def step(i, carry):
        _, slot, _ = slot_of(ca_ref, table_ref, d * convs + i, z)
        place_ref[i] = slot
        for source in range(NX):
            column, slot, which = slot_of(ca_ref, table_ref, (z * NX + source) * convs + i, z)

            @pl.when(column == x)
            def _():
                choice_ref[source * NZ + (slot & (NZ - 1))] = which

        return carry

    lax.fori_loop(0, convs, step, 0)


def rank_kernel(choice_ref, tok_ref, *refs):
    stacks = refs[0:9]
    rank_ref, up_ref = refs[9:11]
    depth = tok_ref.shape[2]
    width = stacks[0].shape[2]
    rows = tok_ref.shape[1]
    for k in range(NZ):
        tok = jnp.concatenate([tok_ref[r * NZ + k] for r in range(NX)], axis=0)
        if k == NZ // 2:
            w = jnp.concatenate([stacks[k][:depth], stacks[NZ][:depth]], axis=1)
        else:
            w = jnp.concatenate([stacks[k][0, :depth], stacks[k][1, :depth]], axis=1)
        res = jnp.dot(tok, w, preferred_element_type=F32)
        for r in range(NX):
            slot = r * NZ + k
            which = choice_ref[slot]
            part = res[r * rows : (r + 1) * rows]
            rank_ref[slot] = jnp.where(which == 1, part[:, width:], part[:, :width]).astype(BF)
            if k == NZ // 2:
                up_ref[slot] = jnp.where(which == 1, stacks[NZ][depth:], stacks[k][depth:])
            else:
                up_ref[slot] = stacks[k][which, depth:]


def unslot_kernel(place_ref, got, keep, send):
    c = lax.axis_index("tensor") & 1
    half = keep.shape[0]
    for j in range(half):
        keep[j] = got[place_ref[c * half + j]]
        send[j] = got[place_ref[(1 - c) * half + j]]


def final_kernel(
    place_ref, span_ref, mine, other, ups, b0, b1, b2, b3, bias, cosine, sine, out
):
    c = lax.axis_index("tensor") & 1
    step = pl.program_id(0)
    half, rows, _ = mine.shape
    rank = mine.shape[2] // 2
    per = out.shape[1] // rows
    head = out.shape[2] // 2
    for j in range(per):
        conv = step * per + j
        here = conv & (half - 1)
        act = jnp.where((conv >> 3) == c, mine[here], other[here])
        up = ups[place_ref[conv]]
        key_delta = jnp.dot(act[:, :rank], up[:rank], preferred_element_type=F32).astype(BF)
        value_delta = jnp.dot(act[:, rank:], up[rank:], preferred_element_type=F32).astype(BF)
        spot = pl.ds(j * rows, rows)
        base = b0[spot].astype(F32) + b1[spot].astype(F32)
        base = base + b2[spot].astype(F32) + b3[spot].astype(F32)
        base = base + bias[0:1].astype(F32)
        key = base[:, :head] + key_delta.astype(F32)
        value = base[:, head:] + value_delta.astype(F32)
        key = key * cosine[spot] + pltpu.roll(key, head // 2, 1) * sine[spot]
        live = lax.broadcasted_iota(jnp.int32, (rows, head), 0) < span_ref[conv]
        out[0, spot, :head] = jnp.where(live, key, 0.0).astype(BF)
        out[0, spot, head:] = jnp.where(live, value, 0.0).astype(BF)


VMEM_SPEC = pl.BlockSpec(memory_space=pltpu.VMEM)
HBM_SPEC = pl.BlockSpec(memory_space=pltpu.HBM)
SMEM_SPEC = pl.BlockSpec(memory_space=pltpu.SMEM)


def body(
    tokens,
    key_value_weight,
    key_value_bias,
    adapter_down_weight,
    adapter_up_weight,
    conversation_adapter,
    adapter_slot_table,
    span_length,
    context_length,
):
    convs = span_length.shape[0]
    total, depth = tokens.shape
    rows = total // convs
    heads, width = key_value_weight.shape[1:]
    head = width // 2
    double_rank = adapter_down_weight.shape[2]
    t = lax.axis_index("tensor")
    y, c = t // NC, t % NC
    half = convs // 2

    stored = adapter_down_weight.shape[0]
    packed = pl.pallas_call(
        pack_kernel,
        out_shape=jax.ShapeDtypeStruct((NX * NZ, rows, depth), BF),
        in_specs=[SMEM_SPEC, SMEM_SPEC, VMEM_SPEC],
        out_specs=HBM_SPEC,
        scratch_shapes=[pltpu.SemaphoreType.DMA],
        compiler_params=pltpu.CompilerParams(vmem_limit_bytes=6 * 1024 * 1024),
        name="pack",
    )(conversation_adapter, adapter_slot_table, tokens.reshape(convs, rows, depth))
    got = exchange_x(packed)
    tokens = lax.optimization_barrier((tokens, packed))[0]
    part = jnp.einsum("td,dhe->hte", tokens, key_value_weight, preferred_element_type=F32)
    part = part.astype(BF).reshape(NY, NC, total, width)
    keep = lax.dynamic_index_in_dim(part, c, 1, keepdims=False)
    send = lax.dynamic_index_in_dim(part, 1 - c, 1, keepdims=False)
    stack = jnp.concatenate(
        [adapter_down_weight, adapter_up_weight.reshape(stored, double_rank, head)], axis=1
    )
    f1, b1 = lax.optimization_barrier((shift_z(stack, 1), shift_z(stack, -1)))
    f2, b2 = lax.optimization_barrier((shift_z(f1, 1), shift_z(b1, -1)))
    f3, b3 = lax.optimization_barrier((shift_z(f2, 1), shift_z(b2, -1)))
    f4, b4 = shift_z(f3[0], 1), shift_z(b3[1], -1)
    stacks = [stack, b1, b2, b3, f4, f3, f2, f1, b4]

    choice, place = pl.pallas_call(
        plan_kernel,
        out_shape=[
            jax.ShapeDtypeStruct((NX * NZ,), jnp.int32),
            jax.ShapeDtypeStruct((convs,), jnp.int32),
        ],
        in_specs=[SMEM_SPEC, SMEM_SPEC],
        out_specs=[SMEM_SPEC, SMEM_SPEC],
        compiler_params=pltpu.CompilerParams(vmem_limit_bytes=1024 * 1024),
        name="plan",
    )(conversation_adapter, adapter_slot_table)

    pair = (keep.astype(F32) + swap_core(send).astype(F32)).astype(BF)
    bases = [lax.dynamic_index_in_dim(pair, (y + s) % NY, 0, keepdims=False) for s in range(NY)]
    bases = [bases[0]] + [shift_y(bases[s], s) for s in range(1, NY)]

    positions = (
        (context_length[:, None] + jnp.arange(rows, dtype=jnp.int32)[None, :])
        .reshape(-1)
        .astype(F32)
    )
    inverse_freq = jnp.exp(
        jnp.arange(head // 2, dtype=F32) * (-2.0 * math.log(rope_base) / head)
    )
    angles = positions[:, None] * inverse_freq[None, :]
    cosine, sine = jnp.cos(angles), jnp.sin(angles)
    cosine = jnp.concatenate([cosine, cosine], axis=-1)
    sine = jnp.concatenate([-sine, sine], axis=-1)

    got, place = lax.optimization_barrier((got, place))
    slots = NX * NZ
    ranks, ups = pl.pallas_call(
        rank_kernel,
        out_shape=[
            jax.ShapeDtypeStruct((slots, rows, double_rank), BF),
            jax.ShapeDtypeStruct((slots, double_rank, head), BF),
        ],
        in_specs=[SMEM_SPEC] + [VMEM_SPEC] * 10,
        out_specs=[VMEM_SPEC] * 2,
        compiler_params=pltpu.CompilerParams(vmem_limit_bytes=12 * 1024 * 1024),
        name="rank",
    )(choice, got, *stacks)
    back = exchange_x(ranks)
    back, bases = lax.optimization_barrier((back, bases))

    kept = jax.ShapeDtypeStruct((half, rows, double_rank), BF)
    keep_r, send_r = pl.pallas_call(
        unslot_kernel,
        out_shape=[kept, kept],
        in_specs=[SMEM_SPEC, VMEM_SPEC],
        out_specs=[VMEM_SPEC] * 2,
        compiler_params=pltpu.CompilerParams(vmem_limit_bytes=4 * 1024 * 1024),
        name="unslot",
    )(place, back)
    mine = (keep_r.astype(F32) + swap_core(send_r).astype(F32)).astype(BF)
    up_back = exchange_x(ups)
    others = [shift_y(mine, s) for s in range(1, NY)]
    others, up_back = lax.optimization_barrier((others, up_back))
    total_rank = mine.astype(F32)
    for o in others:
        total_rank = total_rank + o.astype(F32)
    mine = total_rank.astype(BF)
    other = swap_core(mine)

    steps = 4
    base_spec = pl.BlockSpec((total // steps, width), lambda i, *_: (i, 0))
    trig_spec = pl.BlockSpec((total // steps, head), lambda i, *_: (i, 0))
    full = lambda a: pl.BlockSpec(a.shape, lambda i, *_: (0,) * a.ndim)
    return pl.pallas_call(
        final_kernel,
        out_shape=jax.ShapeDtypeStruct((1, total, width), BF),
        grid_spec=pltpu.PrefetchScalarGridSpec(
            num_scalar_prefetch=2,
            grid=(steps,),
            in_specs=[full(mine), full(other), full(up_back)]
            + [base_spec] * 4
            + [full(key_value_bias), trig_spec, trig_spec],
            out_specs=pl.BlockSpec((1, total // steps, width), lambda i, *_: (0, i, 0)),
        ),
        compiler_params=pltpu.CompilerParams(vmem_limit_bytes=10 * 1024 * 1024),
        name="final",
    )(place, span_length, mine, other, up_back, *bases, key_value_bias, cosine, sine)


def solution(mesh):
    placed = (
        P("dp", "tensor"),
        P("tensor", None, None),
        P("tensor", None),
        P("dp", "tensor", None),
        P("dp", "tensor", None, None, None),
        P(),
        P(),
        P("dp"),
        P("dp"),
    )
    return jax.shard_map(
        body, mesh=mesh, in_specs=placed, out_specs=P("tensor", "dp", None), check_vma=False
    )
```

```python
import functools
import math

import jax
import jax.numpy as jnp
from jax import lax
from jax.experimental import pallas as pl
from jax.experimental.pallas import tpu as pltpu
from jax.sharding import PartitionSpec as P

rope_base = 1000000.0
NZ, NX, NY, NC = 8, 4, 4, 2
BF = jnp.bfloat16
F32 = jnp.float32


def shift_x(v, s):
    pairs = [(z * NX + x, z * NX + (x + s) % NX) for z in range(NZ) for x in range(NX)]
    return lax.ppermute(v, "dp", pairs)


def shift_z(v, s):
    pairs = [(z * NX + x, ((z + s) % NZ) * NX + x) for z in range(NZ) for x in range(NX)]
    return lax.ppermute(v, "dp", pairs)


def shift_y(v, s):
    pairs = [(y * NC + c, ((y + s) % NY) * NC + c) for y in range(NY) for c in range(NC)]
    return lax.ppermute(v, "tensor", pairs)


def swap_core(v):
    return lax.ppermute(v, "tensor", [(t, t ^ 1) for t in range(NY * NC)])


def exchange_x(v):
    groups = [[z * NX + x for x in range(NX)] for z in range(NZ)]
    return lax.all_to_all(v, "dp", 0, 0, tiled=True, axis_index_groups=groups)


def slot_of(ca_ref, table_ref, index, z):
    storage = table_ref[ca_ref[index]]
    owner = storage >> 1
    column = owner & (NX - 1)
    along = ((owner >> 2) - z) & (NZ - 1)
    return column, column * NZ + along, storage & 1


def pack_kernel(ca_ref, table_ref, tok_ref, out_ref, sem):
    d = lax.axis_index("dp")
    convs = tok_ref.shape[0]

    def step(i, carry):
        _, slot, _ = slot_of(ca_ref, table_ref, d * convs + i, d >> 2)
        pltpu.make_async_copy(tok_ref.at[i], out_ref.at[slot], sem).start()
        return carry

    lax.fori_loop(0, convs, step, 0)
    pltpu.make_async_copy(tok_ref, tok_ref, sem).wait()


def plan_kernel(ca_ref, table_ref, choice_ref, place_ref):
    d = lax.axis_index("dp")
    z, x = d >> 2, d & (NX - 1)
    convs = place_ref.shape[0]

    def clear(i, carry):
        choice_ref[i] = 0
        return carry

    lax.fori_loop(0, NX * NZ, clear, 0)

    def step(i, carry):
        column, slot, _ = slot_of(ca_ref, table_ref, d * convs + i, z)
        place_ref[i] = ((column - x) & (NX - 1)) * NZ + (slot & (NZ - 1))
        for source in range(NX):
            column, slot, which = slot_of(ca_ref, table_ref, (z * NX + source) * convs + i, z)

            @pl.when(column == x)
            def _():
                choice_ref[source * NZ + (slot & (NZ - 1))] = which

        return carry

    lax.fori_loop(0, convs, step, 0)


def rank_rows(k, tok_ref, choice_ref, weights, blocks, ranks, ups):
    x = lax.axis_index("dp") & (NX - 1)
    rows = tok_ref.shape[1]
    slots = [((x - r) & (NX - 1)) * NZ + k for r in range(NX)]
    tok = jnp.concatenate([tok_ref[slot] for slot in slots], axis=0)
    width = weights[0].shape[1]
    res = jnp.dot(tok, jnp.concatenate(weights, axis=1), preferred_element_type=F32)
    for r in range(NX):
        second = choice_ref[slots[r]] == 1
        part = res[r * rows : (r + 1) * rows]
        ranks[r][k] = jnp.where(second, part[:, width:], part[:, :width]).astype(BF)
        ups[r][k] = jnp.where(second, blocks[1], blocks[0])


def rank_kernel(choice_ref, tok_ref, own, b1, b2, b3, f3, f2, f1, *refs):
    ranks, ups = refs[0:4], refs[4:8]
    held, sems = refs[8:10]
    depth = tok_ref.shape[2]
    copies = [pltpu.make_async_copy(v, held.at[i], sems.at[i]) for i, v in enumerate((b3, f3))]
    for copy in copies:
        copy.start()
    for k, v in ((0, own), (1, b1), (2, b2), (6, f2), (7, f1), (3, held.at[0]), (5, held.at[1])):
        if k == 3:
            copies[0].wait()
        if k == 5:
            copies[1].wait()
        weights = [v[i, :depth] for i in range(2)]
        rank_rows(k, tok_ref, choice_ref, weights, [v[i, depth:] for i in range(2)], ranks, ups)


def opposite_kernel(choice_ref, tok_ref, f4, b4, *refs):
    ranks, ups = refs[8:12], refs[12:16]
    depth = tok_ref.shape[2]
    x = lax.axis_index("dp") & (NX - 1)
    rows = tok_ref.shape[1]
    tok = jnp.concatenate([tok_ref[(x - r) & (NX - 1)] for r in range(NX)], axis=0)
    weights = jnp.concatenate([f4[:depth], b4[:depth]], axis=1)
    width = f4.shape[1]
    res = jnp.dot(tok, weights, preferred_element_type=F32)
    for r in range(NX):
        second = choice_ref[((x - r) & (NX - 1)) * NZ + NZ // 2] == 1
        part = res[r * rows : (r + 1) * rows]
        ranks[r][0] = jnp.where(second, part[:, width:], part[:, :width]).astype(BF)
        ups[r][0] = jnp.where(second, b4[depth:], f4[depth:])


def pick(sources, place, count):
    across, along = place >> 3, place & (NZ - 1)
    value = sources[0][along]
    for r in range(1, count):
        value = jnp.where(across == r, sources[r][along], value)
    return value


def unslot_kernel(place_ref, g0, g1, g2, g3, keep, send):
    c = lax.axis_index("tensor") & 1
    half = keep.shape[0]
    for j in range(half):
        keep[j] = pick((g0, g1, g2, g3), place_ref[c * half + j], NX)
        send[j] = pick((g0, g1, g2, g3), place_ref[(1 - c) * half + j], NX)


def final_kernel(
    place_ref, span_ref, mine, other, u0, u1, u2, u3, b0, b1, b2, b3, bias, cosine, sine, out
):
    c = lax.axis_index("tensor") & 1
    step = pl.program_id(0)
    half, rows, _ = mine.shape
    rank = mine.shape[2] // 2
    per = out.shape[1] // rows
    head = out.shape[2] // 2
    for j in range(per):
        conv = step * per + j
        here = conv & (half - 1)
        act = jnp.where((conv >> 3) == c, mine[here], other[here])
        up = pick((u0, u1, u2, u3), place_ref[conv], NX)
        key_delta = jnp.dot(act[:, :rank], up[:rank], preferred_element_type=F32).astype(BF)
        value_delta = jnp.dot(act[:, rank:], up[rank:], preferred_element_type=F32).astype(BF)
        spot = pl.ds(j * rows, rows)
        base = b0[spot].astype(F32) + b1[spot].astype(F32)
        base = base + b2[spot].astype(F32) + b3[spot].astype(F32)
        base = base + bias[0:1].astype(F32)
        key = base[:, :head] + key_delta.astype(F32)
        value = base[:, head:] + value_delta.astype(F32)
        key = key * cosine[spot] + pltpu.roll(key, head // 2, 1) * sine[spot]
        live = lax.broadcasted_iota(jnp.int32, (rows, head), 0) < span_ref[conv]
        out[0, spot, :head] = jnp.where(live, key, 0.0).astype(BF)
        out[0, spot, head:] = jnp.where(live, value, 0.0).astype(BF)


VMEM_SPEC = pl.BlockSpec(memory_space=pltpu.VMEM)
ANY_SPEC = pl.BlockSpec(memory_space=pl.ANY)
HBM_SPEC = pl.BlockSpec(memory_space=pltpu.HBM)
SMEM_SPEC = pl.BlockSpec(memory_space=pltpu.SMEM)


def body(
    tokens,
    key_value_weight,
    key_value_bias,
    adapter_down_weight,
    adapter_up_weight,
    conversation_adapter,
    adapter_slot_table,
    span_length,
    context_length,
):
    convs = span_length.shape[0]
    total, depth = tokens.shape
    rows = total // convs
    heads, width = key_value_weight.shape[1:]
    head = width // 2
    double_rank = adapter_down_weight.shape[2]
    t = lax.axis_index("tensor")
    y, c = t // NC, t % NC
    half = convs // 2

    stored = adapter_down_weight.shape[0]
    packed = pl.pallas_call(
        pack_kernel,
        out_shape=jax.ShapeDtypeStruct((NX * NZ, rows, depth), BF),
        in_specs=[SMEM_SPEC, SMEM_SPEC, VMEM_SPEC],
        out_specs=HBM_SPEC,
        scratch_shapes=[pltpu.SemaphoreType.DMA],
        compiler_params=pltpu.CompilerParams(vmem_limit_bytes=60 * 1024 * 1024),
        name="pack",
    )(conversation_adapter, adapter_slot_table, tokens.reshape(convs, rows, depth))
    got = exchange_x(packed)
    stack = jnp.concatenate(
        [adapter_down_weight, adapter_up_weight.reshape(stored, double_rank, head)], axis=1
    )
    f1, b1 = lax.optimization_barrier((shift_z(stack, 1), shift_z(stack, -1)))
    tokens = lax.optimization_barrier((tokens, packed, f1, b1))[0]
    part = jnp.einsum("td,dhe->hte", tokens, key_value_weight, preferred_element_type=F32)
    part = part.astype(BF).reshape(NY, NC, total, width)
    flat = part.reshape(NY * NC, total, width)
    keep, send = [
        [
            lax.dynamic_index_in_dim(flat, (y + s) % NY * NC + core, 0, keepdims=False)
            for s in range(NY)
        ]
        for core in (c, 1 - c)
    ]
    choice, place = pl.pallas_call(
        plan_kernel,
        out_shape=[
            jax.ShapeDtypeStruct((NX * NZ,), jnp.int32),
            jax.ShapeDtypeStruct((convs,), jnp.int32),
        ],
        in_specs=[SMEM_SPEC, SMEM_SPEC],
        out_specs=[SMEM_SPEC, SMEM_SPEC],
        compiler_params=pltpu.CompilerParams(vmem_limit_bytes=1024 * 1024),
        name="plan",
    )(conversation_adapter, adapter_slot_table)

    bases = [(k.astype(F32) + swap_core(v).astype(F32)).astype(BF) for k, v in zip(keep, send)]

    positions = (
        (context_length[:, None] + jnp.arange(rows, dtype=jnp.int32)[None, :])
        .reshape(-1)
        .astype(F32)
    )
    lane = jnp.arange(head, dtype=jnp.int32)
    inverse_freq = jnp.exp(
        (lane % (head // 2)).astype(F32) * (-2.0 * math.log(rope_base) / head)
    )
    angles = positions[:, None] * inverse_freq[None, :]
    cosine = jnp.cos(angles)
    sine = jnp.where(lane < head // 2, -1.0, 1.0) * jnp.sin(angles)

    f2, b2 = lax.optimization_barrier((shift_z(f1, 1), shift_z(b1, -1)))
    f3, b3 = lax.optimization_barrier((shift_z(f2, 1), shift_z(b2, -1)))
    f3_first, b3_second = lax.optimization_barrier((f3[0], b3[1], bases))[:2]
    f4, b4 = shift_z(f3_first, 1), shift_z(b3_second, -1)

    bases = [bases[0]] + [shift_y(bases[s], s) for s in range(1, NY)]
    choice = lax.optimization_barrier((choice, place))[0]
    small = jax.ShapeDtypeStruct((NZ, rows, double_rank), BF)
    blocks = jax.ShapeDtypeStruct((NZ, double_rank, head), BF)
    results = pl.pallas_call(
        rank_kernel,
        out_shape=[small] * NX + [blocks] * NX,
        in_specs=[SMEM_SPEC] + [VMEM_SPEC] * 4 + [ANY_SPEC] * 2 + [VMEM_SPEC] * 2,
        out_specs=[VMEM_SPEC] * 8,
        scratch_shapes=[
            pltpu.VMEM((2, *stack.shape), BF),
            pltpu.SemaphoreType.DMA((2,)),
        ],
        compiler_params=pltpu.CompilerParams(vmem_limit_bytes=12 * 1024 * 1024),
        name="rank",
    )(choice, got, stack, b1, b2, b3, f3, f2, f1)
    opposite = NZ // 2
    whole = lambda n: pl.BlockSpec(memory_space=pltpu.VMEM)
    one = lambda a: pl.BlockSpec((1, *a.shape[1:]), lambda i: (opposite,) + (0,) * (a.ndim - 1))
    tok_spec = pl.BlockSpec((NX, pl.Squeezed(), rows, depth), lambda i: (0, opposite, 0, 0))
    results = pl.pallas_call(
        opposite_kernel,
        grid=(1,),
        out_shape=[small] * NX + [blocks] * NX,
        in_specs=[SMEM_SPEC, tok_spec, whole(0), whole(0)] + [ANY_SPEC] * 8,
        out_specs=[one(v) for v in results],
        input_output_aliases={4 + i: i for i in range(8)},
        compiler_params=pltpu.CompilerParams(vmem_limit_bytes=6 * 1024 * 1024),
        name="opposite",
    )(choice, got.reshape(NX, NZ, rows, depth), f4, b4, *results)
    ranks, ups = results[:NX], results[NX:]
    back = [ranks[0]] + [shift_x(ranks[r], -r) for r in range(1, NX)]
    back = lax.optimization_barrier((back, bases))[0]

    kept = jax.ShapeDtypeStruct((half, rows, double_rank), BF)
    keep_r, send_r = pl.pallas_call(
        unslot_kernel,
        out_shape=[kept, kept],
        in_specs=[SMEM_SPEC] + [VMEM_SPEC] * 4,
        out_specs=[VMEM_SPEC] * 2,
        compiler_params=pltpu.CompilerParams(vmem_limit_bytes=4 * 1024 * 1024),
        name="unslot",
    )(place, *back)
    mine = (keep_r.astype(F32) + swap_core(send_r).astype(F32)).astype(BF)
    up_back = [ups[0]] + [shift_x(ups[r], -r) for r in range(1, NX)]
    others = [shift_y(mine, s) for s in range(1, NY)]
    others, up_back = lax.optimization_barrier((others, up_back))
    total_rank = mine.astype(F32)
    for o in others:
        total_rank = total_rank + o.astype(F32)
    mine = total_rank.astype(BF)
    other = swap_core(mine)

    steps = 4
    base_spec = pl.BlockSpec((total // steps, width), lambda i, *_: (i, 0))
    trig_spec = pl.BlockSpec((total // steps, head), lambda i, *_: (i, 0))
    full = lambda a: pl.BlockSpec(a.shape, lambda i, *_: (0,) * a.ndim)
    return pl.pallas_call(
        final_kernel,
        out_shape=jax.ShapeDtypeStruct((1, total, width), BF),
        grid_spec=pltpu.PrefetchScalarGridSpec(
            num_scalar_prefetch=2,
            grid=(steps,),
            in_specs=[full(mine), full(other)]
            + [full(u) for u in up_back]
            + [base_spec] * 4
            + [full(key_value_bias), trig_spec, trig_spec],
            out_specs=pl.BlockSpec((1, total // steps, width), lambda i, *_: (0, i, 0)),
        ),
        compiler_params=pltpu.CompilerParams(vmem_limit_bytes=10 * 1024 * 1024),
        name="final",
    )(place, span_length, mine, other, *up_back, *bases, key_value_bias, cosine, sine)


def solution(mesh):
    placed = (
        P("dp", "tensor"),
        P("tensor", None, None),
        P("tensor", None),
        P("dp", "tensor", None),
        P("dp", "tensor", None, None, None),
        P(),
        P(),
        P("dp"),
        P("dp"),
    )
    return jax.shard_map(
        body, mesh=mesh, in_specs=placed, out_specs=P("tensor", "dp", None), check_vma=False
    )
```

```python
import functools
import math

import jax
import jax.numpy as jnp
from jax import lax
from jax.experimental import pallas as pl
from jax.experimental.pallas import tpu as pltpu
from jax.sharding import PartitionSpec as P

rope_base = 1000000.0
NZ, NX, NY, NC = 8, 4, 4, 2
BF = jnp.bfloat16
F32 = jnp.float32


def shift_x(v, s):
    pairs = [(z * NX + x, z * NX + (x + s) % NX) for z in range(NZ) for x in range(NX)]
    return lax.ppermute(v, "dp", pairs)


def shift_z(v, s):
    pairs = [(z * NX + x, ((z + s) % NZ) * NX + x) for z in range(NZ) for x in range(NX)]
    return lax.ppermute(v, "dp", pairs)


def shift_y(v, s):
    pairs = [(y * NC + c, ((y + s) % NY) * NC + c) for y in range(NY) for c in range(NC)]
    return lax.ppermute(v, "tensor", pairs)


def swap_core(v):
    return lax.ppermute(v, "tensor", [(t, t ^ 1) for t in range(NY * NC)])


def exchange_x(v):
    groups = [[z * NX + x for x in range(NX)] for z in range(NZ)]
    return lax.all_to_all(v, "dp", 0, 0, tiled=True, axis_index_groups=groups)


def slot_of(ca_ref, table_ref, index, z):
    storage = table_ref[ca_ref[index]]
    owner = storage >> 1
    column = owner & (NX - 1)
    along = ((owner >> 2) - z) & (NZ - 1)
    return column, column * NZ + along, storage & 1


def pack_kernel(ca_ref, table_ref, tok_ref, out_ref, sem):
    d = lax.axis_index("dp")
    convs = tok_ref.shape[0]

    def step(i, carry):
        _, slot, _ = slot_of(ca_ref, table_ref, d * convs + i, d >> 2)
        pltpu.make_async_copy(tok_ref.at[i], out_ref.at[slot], sem).start()
        return carry

    lax.fori_loop(0, convs, step, 0)
    pltpu.make_async_copy(tok_ref, tok_ref, sem).wait()


def plan_kernel(ca_ref, table_ref, choice_ref, place_ref):
    d = lax.axis_index("dp")
    z, x = d >> 2, d & (NX - 1)
    convs = place_ref.shape[0]

    def clear(i, carry):
        choice_ref[i] = 0
        return carry

    lax.fori_loop(0, NX * NZ, clear, 0)

    def step(i, carry):
        column, slot, _ = slot_of(ca_ref, table_ref, d * convs + i, z)
        place_ref[i] = ((column - x) & (NX - 1)) * NZ + (slot & (NZ - 1))
        for source in range(NX):
            column, slot, which = slot_of(ca_ref, table_ref, (z * NX + source) * convs + i, z)

            @pl.when(column == x)
            def _():
                choice_ref[source * NZ + (slot & (NZ - 1))] = which

        return carry

    lax.fori_loop(0, convs, step, 0)


def rank_rows(k, tok_ref, choice_ref, weights, blocks, ranks, ups):
    x = lax.axis_index("dp") & (NX - 1)
    rows = tok_ref.shape[1]
    slots = [((x - r) & (NX - 1)) * NZ + k for r in range(NX)]
    tok = jnp.concatenate([tok_ref[slot] for slot in slots], axis=0)
    width = weights[0].shape[1]
    res = jnp.dot(tok, jnp.concatenate(weights, axis=1), preferred_element_type=F32)
    for r in range(NX):
        second = choice_ref[slots[r]] == 1
        part = res[r * rows : (r + 1) * rows]
        ranks[r][k] = jnp.where(second, part[:, width:], part[:, :width]).astype(BF)
        ups[r][k] = jnp.where(second, blocks[1], blocks[0])


def rank_kernel(choice_ref, tok_ref, own, b1, b2, b3, f3, f2, f1, *refs):
    ranks, ups = refs[0:4], refs[4:8]
    held, sems = refs[8:10]
    depth = tok_ref.shape[2]
    copies = [pltpu.make_async_copy(v, held.at[i], sems.at[i]) for i, v in enumerate((b3, f3))]
    for copy in copies:
        copy.start()
    for k, v in ((0, own), (1, b1), (2, b2), (6, f2), (7, f1), (3, held.at[0]), (5, held.at[1])):
        if k == 3:
            copies[0].wait()
        if k == 5:
            copies[1].wait()
        weights = [v[i, :depth] for i in range(2)]
        rank_rows(k, tok_ref, choice_ref, weights, [v[i, depth:] for i in range(2)], ranks, ups)


def opposite_kernel(choice_ref, tok_ref, f4, b4, *refs):
    ranks, ups = refs[8:12], refs[12:16]
    depth = tok_ref.shape[2]
    x = lax.axis_index("dp") & (NX - 1)
    rows = tok_ref.shape[1]
    tok = jnp.concatenate([tok_ref[(x - r) & (NX - 1)] for r in range(NX)], axis=0)
    weights = jnp.concatenate([f4[:depth], b4[:depth]], axis=1)
    width = f4.shape[1]
    res = jnp.dot(tok, weights, preferred_element_type=F32)
    for r in range(NX):
        second = choice_ref[((x - r) & (NX - 1)) * NZ + NZ // 2] == 1
        part = res[r * rows : (r + 1) * rows]
        ranks[r][0] = jnp.where(second, part[:, width:], part[:, :width]).astype(BF)
        ups[r][0] = jnp.where(second, b4[depth:], f4[depth:])


def pick(sources, place, count):
    across, along = place >> 3, place & (NZ - 1)
    value = sources[0][along]
    for r in range(1, count):
        value = jnp.where(across == r, sources[r][along], value)
    return value


def unslot_kernel(place_ref, g0, g1, g2, g3, keep, send):
    c = lax.axis_index("tensor") & 1
    half = keep.shape[0]
    for j in range(half):
        keep[j] = pick((g0, g1, g2, g3), place_ref[c * half + j], NX)
        send[j] = pick((g0, g1, g2, g3), place_ref[(1 - c) * half + j], NX)


def final_kernel(
    place_ref, span_ref, mine, other, u0, u1, u2, u3, b0, b1, b2, b3, bias, cosine, sine, out
):
    c = lax.axis_index("tensor") & 1
    step = pl.program_id(0)
    half, rows, _ = mine.shape
    rank = mine.shape[2] // 2
    per = out.shape[1] // rows
    head = out.shape[2] // 2
    for j in range(per):
        conv = step * per + j
        here = conv & (half - 1)
        act = jnp.where((conv >> 3) == c, mine[here], other[here])
        up = pick((u0, u1, u2, u3), place_ref[conv], NX)
        key_delta = jnp.dot(act[:, :rank], up[:rank], preferred_element_type=F32).astype(BF)
        value_delta = jnp.dot(act[:, rank:], up[rank:], preferred_element_type=F32).astype(BF)
        spot = pl.ds(j * rows, rows)
        base = b0[spot].astype(F32) + b1[spot].astype(F32)
        base = base + b2[spot].astype(F32) + b3[spot].astype(F32)
        base = base + bias[0:1].astype(F32)
        key = base[:, :head] + key_delta.astype(F32)
        value = base[:, head:] + value_delta.astype(F32)
        key = key * cosine[spot] + pltpu.roll(key, head // 2, 1) * sine[spot]
        live = lax.broadcasted_iota(jnp.int32, (rows, head), 0) < span_ref[conv]
        out[0, spot, :head] = jnp.where(live, key, 0.0).astype(BF)
        out[0, spot, head:] = jnp.where(live, value, 0.0).astype(BF)


VMEM_SPEC = pl.BlockSpec(memory_space=pltpu.VMEM)
ANY_SPEC = pl.BlockSpec(memory_space=pl.ANY)
HBM_SPEC = pl.BlockSpec(memory_space=pltpu.HBM)
SMEM_SPEC = pl.BlockSpec(memory_space=pltpu.SMEM)


def body(
    tokens,
    key_value_weight,
    key_value_bias,
    adapter_down_weight,
    adapter_up_weight,
    conversation_adapter,
    adapter_slot_table,
    span_length,
    context_length,
):
    convs = span_length.shape[0]
    total, depth = tokens.shape
    rows = total // convs
    heads, width = key_value_weight.shape[1:]
    head = width // 2
    double_rank = adapter_down_weight.shape[2]
    t = lax.axis_index("tensor")
    y, c = t // NC, t % NC
    half = convs // 2

    stored = adapter_down_weight.shape[0]
    packed = pl.pallas_call(
        pack_kernel,
        out_shape=jax.ShapeDtypeStruct((NX * NZ, rows, depth), BF),
        in_specs=[SMEM_SPEC, SMEM_SPEC, VMEM_SPEC],
        out_specs=HBM_SPEC,
        scratch_shapes=[pltpu.SemaphoreType.DMA],
        compiler_params=pltpu.CompilerParams(vmem_limit_bytes=60 * 1024 * 1024),
        name="pack",
    )(conversation_adapter, adapter_slot_table, tokens.reshape(convs, rows, depth))
    got = exchange_x(packed)
    stack = jnp.concatenate(
        [adapter_down_weight, adapter_up_weight.reshape(stored, double_rank, head)], axis=1
    )
    f1, b1 = lax.optimization_barrier((shift_z(stack, 1), shift_z(stack, -1)))
    tokens = lax.optimization_barrier((tokens, packed, f1, b1))[0]
    part = jnp.einsum("td,dhe->hte", tokens, key_value_weight, preferred_element_type=F32)
    part = part.astype(BF).reshape(NY, NC, total, width)
    flat = part.reshape(NY * NC, total, width)
    keep, send = [
        [
            lax.dynamic_index_in_dim(flat, (y + s) % NY * NC + core, 0, keepdims=False)
            for s in range(NY)
        ]
        for core in (c, 1 - c)
    ]
    choice, place = pl.pallas_call(
        plan_kernel,
        out_shape=[
            jax.ShapeDtypeStruct((NX * NZ,), jnp.int32),
            jax.ShapeDtypeStruct((convs,), jnp.int32),
        ],
        in_specs=[SMEM_SPEC, SMEM_SPEC],
        out_specs=[SMEM_SPEC, SMEM_SPEC],
        compiler_params=pltpu.CompilerParams(vmem_limit_bytes=1024 * 1024),
        name="plan",
    )(conversation_adapter, adapter_slot_table)

    bases = [(k.astype(F32) + swap_core(v).astype(F32)).astype(BF) for k, v in zip(keep, send)]

    positions = (
        (context_length[:, None] + jnp.arange(rows, dtype=jnp.int32)[None, :])
        .reshape(-1)
        .astype(F32)
    )
    lane = jnp.arange(head, dtype=jnp.int32)
    inverse_freq = jnp.exp(
        (lane % (head // 2)).astype(F32) * (-2.0 * math.log(rope_base) / head)
    )
    angles = positions[:, None] * inverse_freq[None, :]
    cosine = jnp.cos(angles)
    sine = jnp.where(lane < head // 2, -1.0, 1.0) * jnp.sin(angles)

    f2, b2 = lax.optimization_barrier((shift_z(f1, 1), shift_z(b1, -1)))
    f3, b3 = lax.optimization_barrier((shift_z(f2, 1), shift_z(b2, -1)))
    f3_first, b3_second = lax.optimization_barrier((f3[0], b3[1], bases))[:2]
    f4, b4 = shift_z(f3_first, 1), shift_z(b3_second, -1)

    bases = [bases[0]] + [shift_y(bases[s], s) for s in range(1, NY)]
    choice = lax.optimization_barrier((choice, place))[0]
    small = jax.ShapeDtypeStruct((NZ, rows, double_rank), BF)
    blocks = jax.ShapeDtypeStruct((NZ, double_rank, head), BF)
    results = pl.pallas_call(
        rank_kernel,
        out_shape=[small] * NX + [blocks] * NX,
        in_specs=[SMEM_SPEC] + [VMEM_SPEC] * 4 + [ANY_SPEC] * 2 + [VMEM_SPEC] * 2,
        out_specs=[VMEM_SPEC] * 8,
        scratch_shapes=[
            pltpu.VMEM((2, *stack.shape), BF),
            pltpu.SemaphoreType.DMA((2,)),
        ],
        compiler_params=pltpu.CompilerParams(vmem_limit_bytes=12 * 1024 * 1024),
        name="rank",
    )(choice, got, stack, b1, b2, b3, f3, f2, f1)
    opposite = NZ // 2
    whole = lambda n: pl.BlockSpec(memory_space=pltpu.VMEM)
    one = lambda a: pl.BlockSpec((1, *a.shape[1:]), lambda i: (opposite,) + (0,) * (a.ndim - 1))
    tok_spec = pl.BlockSpec((NX, pl.Squeezed(), rows, depth), lambda i: (0, opposite, 0, 0))
    results = pl.pallas_call(
        opposite_kernel,
        grid=(1,),
        out_shape=[small] * NX + [blocks] * NX,
        in_specs=[SMEM_SPEC, tok_spec, whole(0), whole(0)] + [ANY_SPEC] * 8,
        out_specs=[one(v) for v in results],
        input_output_aliases={4 + i: i for i in range(8)},
        compiler_params=pltpu.CompilerParams(vmem_limit_bytes=6 * 1024 * 1024),
        name="opposite",
    )(choice, got.reshape(NX, NZ, rows, depth), f4, b4, *results)
    ranks, ups = results[:NX], results[NX:]
    back = [ranks[0]] + [shift_x(ranks[r], -r) for r in range(1, NX)]
    back = lax.optimization_barrier((back, bases))[0]

    kept = jax.ShapeDtypeStruct((half, rows, double_rank), BF)
    keep_r, send_r = pl.pallas_call(
        unslot_kernel,
        out_shape=[kept, kept],
        in_specs=[SMEM_SPEC] + [VMEM_SPEC] * 4,
        out_specs=[VMEM_SPEC] * 2,
        compiler_params=pltpu.CompilerParams(vmem_limit_bytes=4 * 1024 * 1024),
        name="unslot",
    )(place, *back)
    mine = (keep_r.astype(F32) + swap_core(send_r).astype(F32)).astype(BF)
    up_back = [ups[0]] + [shift_x(ups[r], -r) for r in range(1, NX)]
    others = [shift_y(mine, s) for s in range(1, NY)]
    others, up_back = lax.optimization_barrier((others, up_back))
    total_rank = mine.astype(F32)
    for o in others:
        total_rank = total_rank + o.astype(F32)
    mine = total_rank.astype(BF)
    other = swap_core(mine)

    steps = 2
    base_spec = pl.BlockSpec((total // steps, width), lambda i, *_: (i, 0))
    trig_spec = pl.BlockSpec((total // steps, head), lambda i, *_: (i, 0))
    full = lambda a: pl.BlockSpec(a.shape, lambda i, *_: (0,) * a.ndim)
    return pl.pallas_call(
        final_kernel,
        out_shape=jax.ShapeDtypeStruct((1, total, width), BF),
        grid_spec=pltpu.PrefetchScalarGridSpec(
            num_scalar_prefetch=2,
            grid=(steps,),
            in_specs=[full(mine), full(other)]
            + [full(u) for u in up_back]
            + [base_spec] * 4
            + [full(key_value_bias), trig_spec, trig_spec],
            out_specs=pl.BlockSpec((1, total // steps, width), lambda i, *_: (0, i, 0)),
        ),
        compiler_params=pltpu.CompilerParams(vmem_limit_bytes=10 * 1024 * 1024),
        name="final",
    )(place, span_length, mine, other, *up_back, *bases, key_value_bias, cosine, sine)


def solution(mesh):
    placed = (
        P("dp", "tensor"),
        P("tensor", None, None),
        P("tensor", None),
        P("dp", "tensor", None),
        P("dp", "tensor", None, None, None),
        P(),
        P(),
        P("dp"),
        P("dp"),
    )
    return jax.shard_map(
        body, mesh=mesh, in_specs=placed, out_specs=P("tensor", "dp", None), check_vma=False
    )
```
